768 devices in a mesh: ctx: 192 (over x, y, z_hi, core), tp: 4 (over z_lo).
Axes of the slice: x: 4, y: 8, z: 12 (z_hi: 3, z_lo: 4; z = z_hi * 4 + z_lo), core: 2. Of those that a mesh axis runs over, the one named last changes fastest.
Arguments:
- queries: bfloat16 [49152, 2048], P('ctx', 'tp'), may hold values from -70 to 70
- keys: bfloat16 [49152, 1024], P('ctx', 'tp'), may hold values from -6 to 6
- values: bfloat16 [49152, 1024], P('ctx', 'tp'), may hold values from -6 to 6
- grad_out: bfloat16 [49152, 5376], P(('ctx', 'tp')), may hold values from -24 to 24
- out_weight: bfloat16 [2048, 5376], P('tp'), may hold values from -0.078125 to 0.078125
Outputs:
- grad_queries: float32 [49152, 2048], P('ctx', 'tp')
- grad_keys: float32 [49152, 1024], P('ctx', 'tp')
- grad_values: float32 [49152, 1024], P('ctx', 'tp')
The draws below stay inside these ranges and needn't reach their ends.
All inputs are finite; a program needn't handle non-finite values.
Results may differ from the reference program's by a relative error of at most 0.014.
Values may be sent and summed in bfloat16 or wider, within the bound.
A program may use at most 64 MiB of HBM per device.

```python
import jax
import jax.numpy as jnp
from jax import lax

D = 5376
HQ = 16
KV = 8
HD = 128
WIN = 1024
SEQ_DEV = 256
TOKENS = 49152


def drawn_pair(key):
    query_seed = jax.random.fold_in(key, 101)
    key_seed = jax.random.fold_in(key, 202)
    base_query = jnp.clip(jax.random.normal(query_seed, (TOKENS, HQ * HD), jnp.float32), -6.0, 6.0)
    base_key = jnp.clip(jax.random.normal(key_seed, (TOKENS, KV * HD), jnp.float32), -6.0, 6.0)
    return (base_query, base_key)


def draw_queries(key, part):
    return drawn_pair(key)[0].astype(jnp.bfloat16)


def draw_keys(key, part):
    return drawn_pair(key)[1].astype(jnp.bfloat16)


def level_of(stream_key, extent, split, low, high):
    gain = 1.0
    for dim, shards_of in split:
        steps = jax.random.uniform(jax.random.fold_in(jax.random.fold_in(stream_key, 6), dim), (shards_of,), jnp.float32, low / len(split), high / len(split))
        gain = gain * jnp.repeat(jnp.exp(steps), extent[dim] // shards_of).reshape((-1,) + (1,) * (len(extent) - 1 - dim))
    return gain


def noise(key, dims, scale, bound, shards=(), kind=jnp.bfloat16):
    drawn = scale * jax.random.normal(key, dims, jnp.float32)
    if shards:
        drawn = drawn * level_of(key, dims, shards, -0.22, 0.18)
    return jnp.clip(drawn, -bound, bound).astype(kind)


def setup_inputs(seed: int = 0) -> dict:
    streams_of = jax.random.split(jax.random.key(seed), 6)
    queries = draw_queries(jax.random.fold_in(streams_of[5], 71), 0)
    keys = draw_keys(jax.random.fold_in(streams_of[5], 71), 0)
    values = noise(streams_of[2], (TOKENS, KV * HD), 1.0, 6.0, ((0, 192), (1, 4)))
    grad_out = noise(streams_of[3], (TOKENS, D), 4.0, 24.0, ((0, 768),))
    out_weight = noise(streams_of[4], (HQ * HD, D), D ** -0.5, 0.078125, ((0, 4),))
    return dict(queries=queries, keys=keys, values=values, grad_out=grad_out, out_weight=out_weight)


score_scale = 168.0 ** -0.5


def band_grads(query_block, dout_block, key_span, value_span, query_pos, key_pos):
    shard_rows = query_block.shape[0]
    span_rows = key_span.shape[0]
    kv_heads = KV
    group_size = HQ // KV
    query_heads = query_block.astype(jnp.float32).reshape(shard_rows, kv_heads, group_size, HD)
    dout_heads = dout_block.astype(jnp.float32).reshape(shard_rows, kv_heads, group_size, HD)
    key_heads = key_span.astype(jnp.float32).reshape(span_rows, kv_heads, HD)
    value_heads = value_span.astype(jnp.float32).reshape(span_rows, kv_heads, HD)
    scores = jnp.einsum('sgrd,egd->grse', query_heads, key_heads) * score_scale
    allowed = (key_pos[None, :] <= query_pos[:, None]) & (key_pos[None, :] > query_pos[:, None] - WIN) & (key_pos[None, :] >= 0)
    scores = jnp.where(allowed, scores, -1e30)
    row_max = jnp.max(scores, axis=-1, keepdims=True)
    weights = jnp.where(allowed, jnp.exp(scores - row_max), 0.0)
    probability = weights / jnp.sum(weights, axis=-1, keepdims=True)
    dprobs = jnp.einsum('sgrd,egd->grse', dout_heads, value_heads)
    row_delta = jnp.sum(probability * dprobs, axis=-1, keepdims=True)
    dscores = probability * (dprobs - row_delta)
    probs_low = probability.astype(jnp.bfloat16).astype(jnp.float32)
    dscores_low = dscores.astype(jnp.bfloat16).astype(jnp.float32)
    grad_value = jnp.einsum('grse,sgrd->egd', probs_low, dout_heads)
    grad_query = score_scale * jnp.einsum('grse,egd->sgrd', dscores_low, key_heads)
    grad_key = score_scale * jnp.einsum('grse,sgrd->egd', dscores_low, query_heads)
    return (grad_query.reshape(shard_rows, -1), grad_key.reshape(span_rows, -1),
            grad_value.reshape(span_rows, -1))


def round_earlier(span_terms):
    earlier = lax.optimization_barrier(span_terms[:WIN].astype(jnp.bfloat16)).astype(jnp.float32)
    return jnp.concatenate([earlier, span_terms[WIN:]], axis=0)


def reference(queries, keys, values, grad_out, out_weight):
    dout = jnp.dot(grad_out, out_weight.T, preferred_element_type=jnp.float32).astype(jnp.bfloat16)
    kv_width = keys.shape[1]
    leading = jnp.zeros((WIN, kv_width), keys.dtype)
    key_padded = jnp.concatenate([leading, keys], axis=0)
    value_padded = jnp.concatenate([leading, values], axis=0)
    span_rows = WIN + SEQ_DEV

    def step(carry, block_index):
        key_total, value_total = carry
        start = (block_index * SEQ_DEV).astype(jnp.int32)
        query_block = lax.dynamic_slice_in_dim(queries, start, SEQ_DEV, 0)
        dout_block = lax.dynamic_slice_in_dim(dout, start, SEQ_DEV, 0)
        key_span = lax.dynamic_slice_in_dim(key_padded, start, span_rows, 0)
        value_span = lax.dynamic_slice_in_dim(value_padded, start, span_rows, 0)
        query_pos = start + jnp.arange(SEQ_DEV, dtype=jnp.int32)
        key_pos = start - WIN + jnp.arange(span_rows, dtype=jnp.int32)
        grad_query, grad_key, grad_value = band_grads(query_block, dout_block, key_span, value_span, query_pos, key_pos)
        grad_key = round_earlier(grad_key)
        grad_value = round_earlier(grad_value)
        key_total = lax.dynamic_update_slice_in_dim(
            key_total, lax.dynamic_slice_in_dim(key_total, start, span_rows, 0) + grad_key, start, 0)
        value_total = lax.dynamic_update_slice_in_dim(
            value_total, lax.dynamic_slice_in_dim(value_total, start, span_rows, 0) + grad_value, start, 0)
        return (key_total, value_total), grad_query

    initial = (jnp.zeros((TOKENS + WIN, kv_width), jnp.float32), jnp.zeros((TOKENS + WIN, kv_width), jnp.float32))
    (key_total, value_total), grad_queries = lax.scan(step, initial, jnp.arange(TOKENS // SEQ_DEV, dtype=jnp.int32))
    return grad_queries.reshape(TOKENS, HQ * HD), key_total[WIN:], value_total[WIN:]
```

```python
import functools

import jax
import jax.numpy as jnp
from jax import lax
from jax.experimental import pallas as pl
from jax.experimental.pallas import tpu as pltpu
from jax.sharding import PartitionSpec as P

HD = 128
WIN = 1024
SCALE = 168.0 ** (-0.5)
LOG2E = 1.4426950408889634
NEG = -1e30
MESH = pl.DeviceIdType.MESH
ZHI, ZLO = 3, 4
F32 = jnp.float32
BF16 = jnp.bfloat16

ROWS = (
    ((96, 0, 160), (0, 160, 96), -1),
    ((32, 0, 224), (0, 224, 32), -1),
    ((0, 32, 224), (224, 0, 32), 1),
    ((0, 96, 160), (160, 0, 96), 1),
)


def dot_nt(a, b):
    return lax.dot_general(a, b, (((1,), (1,)), ((), ())), preferred_element_type=F32)


def dot_nn(a, b):
    return lax.dot_general(a, b, (((1,), (0,)), ((), ())), preferred_element_type=F32)


def dot_tn(a, b):
    return lax.dot_general(a, b, (((0,), (0,)), ((), ())), preferred_element_type=F32)


def kernel(
    chips, q_in, k_in, v_in, g_in, w_in, gq_out, gk_out, gv_out,
    main, relay, wbuf, ybuf, dobuf, qbuf, kvbuf, pbuf, dpbuf, dsbuf, stats,
    gsend, grecv, ownf, pbase, ost, dqx,
    loc, ag_s, ag_r, kv_s, kv_r, q_s, q_r, do_s, do_r, gr_s, gr_r, fin_s, fin_r,
):
    ctx = lax.axis_index("ctx")
    k = lax.axis_index("tp")
    e = lax.rem(ctx, 2)
    f = 1 - e
    c = ctx // 2
    r = c // ZHI
    zh = lax.rem(c, ZHI)
    z = zh * ZLO + k
    nz = ZHI * ZLO

    def plane(d):
        zz = lax.rem(z + d + nz, nz)
        return (((r * ZHI + zz // ZLO) * 2 + e), lax.rem(zz, ZLO))

    def group(d, core):
        return ((r * ZHI + lax.rem(zh + d + ZHI, ZHI)) * 2 + core, k)

    def chip(d, core):
        return (lax.rem(c + d + chips, chips) * 2 + core, k)

    partner = (c * 2 + f, k)

    def remote(src, dst, ss, rs, dev):
        return pltpu.make_async_remote_copy(
            src_ref=src, dst_ref=dst, send_sem=ss, recv_sem=rs, device_id=dev, device_id_type=MESH
        )

    def arrive(dst, rs):
        remote(dst, dst, rs, rs, partner).wait_recv()

    def lane(i, n):
        return pl.ds(pl.multiple_of(i * n, n), n)

    local = [
        pltpu.make_async_copy(g_in, main.at[64:128], loc.at[0]),
        pltpu.make_async_copy(w_in, wbuf, loc.at[1]),
        pltpu.make_async_copy(k_in.at[:, lane(e, 128)], kvbuf.at[0, 4 + e], loc.at[2]),
        pltpu.make_async_copy(v_in.at[:, lane(e, 128)], kvbuf.at[1, 4 + e], loc.at[3]),
        pltpu.make_async_copy(q_in.at[:, lane(e, 256)], qbuf.at[e], loc.at[4]),
    ]
    for copy in local:
        copy.start()

    barrier = pltpu.get_barrier_semaphore()

    def greet(dev):
        pl.semaphore_signal(barrier, inc=1, device_id=dev, device_id_type=MESH)

    back = jnp.where(k < 2, 1, -1)
    greet(partner)
    greet(plane(1))
    greet(plane(-1))
    for core in range(2):
        greet(group(back, core))
        for d in (1, 2, -1, -2):
            greet(chip(d, core))
    pl.semaphore_wait(barrier, 13)

    sends = []

    def send(*args):
        copy = remote(*args)
        copy.start()
        sends.append(copy)

    send(g_in.at[32:64], main.at[32:64], ag_s.at[0], ag_r.at[0], plane(1))
    send(g_in.at[0:32], main.at[128:160], ag_s.at[1], ag_r.at[1], plane(-1))
    send(g_in.at[0:32], main.at[0:32], ag_s.at[2], ag_r.at[2], plane(1))
    send(g_in.at[32:64], main.at[160:192], ag_s.at[3], ag_r.at[3], plane(-1))
    send(q_in.at[:, lane(f, 256)], qbuf.at[e], q_s.at[0], q_r.at[0], partner)
    send(k_in.at[:, lane(f, 128)], kvbuf.at[0, 4 + e], kv_s.at[0], kv_r.at[0], partner)
    send(v_in.at[:, lane(f, 128)], kvbuf.at[1, 4 + e], kv_s.at[1], kv_r.at[1], partner)
    arrive(main.at[32:64], ag_r.at[0])
    send(main.at[32:64], relay.at[0:32], ag_s.at[4], ag_r.at[4], plane(1))
    arrive(main.at[128:160], ag_r.at[1])
    send(main.at[128:160], relay.at[32:64], ag_s.at[5], ag_r.at[5], plane(-1))
    for d in (1, 2):
        for core in range(2):
            for which, src in ((0, k_in), (1, v_in)):
                slot = 2 + (d - 1) * 4 + which
                send(
                    src.at[:, 128 * core : 128 * core + 128],
                    kvbuf.at[which, 4 - 2 * d + e],
                    kv_s.at[slot + 2 * core],
                    kv_r.at[slot + 2 * e],
                    chip(d, core),
                )

    for copy in local:
        copy.wait()
    arrive(main.at[0:32], ag_r.at[2])
    arrive(main.at[160:192], ag_r.at[3])
    for h in range(2):
        ybuf[h, 32:224] = dot_nt(main[...], wbuf[256 * h : 256 * h + 256]).astype(BF16)
    arrive(relay.at[0:32], ag_r.at[4])
    arrive(relay.at[32:64], ag_r.at[5])
    for h in range(2):
        ends = dot_nt(relay[...], wbuf[256 * h : 256 * h + 256]).astype(BF16)
        ybuf[h, 0:32] = ends[0:32]
        ybuf[h, 224:256] = ends[32:64]

    for case, (kept, moved, way) in enumerate(ROWS):
        src, home, count = kept
        msrc, mhome, mcount = moved

        def rows_out():
            copies = [
                remote(
                    ybuf.at[core, msrc : msrc + mcount],
                    dobuf.at[e, mhome : mhome + mcount],
                    do_s.at[1 + core],
                    do_r.at[1 + e],
                    group(way, core),
                )
                for core in range(2)
            ]
            copies.append(
                remote(
                    ybuf.at[f, src : src + count],
                    dobuf.at[e, home : home + count],
                    do_s.at[0],
                    do_r.at[0],
                    partner,
                )
            )
            return copies

        @pl.when(k == case)
        def _():
            for copy in rows_out():
                copy.start()
            own = pltpu.make_async_copy(
                ybuf.at[e, src : src + count], dobuf.at[e, home : home + count], loc.at[5]
            )
            own.start()
            own.wait()
            arrive(dobuf.at[f, home : home + count], do_r.at[0])
            for core in range(2):
                arrive(dobuf.at[core, mhome : mhome + mcount], do_r.at[1 + core])
            for copy in rows_out():
                copy.wait_send()

    arrive(qbuf.at[f], q_r.at[0])
    for which in range(2):
        arrive(kvbuf.at[which, 4 + f], kv_r.at[which])
    for d in (1, 2):
        for core in range(2):
            for which in range(2):
                arrive(
                    kvbuf.at[which, 4 - 2 * d + core], kv_r.at[2 + (d - 1) * 4 + which + 2 * core]
                )

    key_row = lax.broadcasted_iota(jnp.int32, (256, 256), 0)
    query_col = lax.broadcasted_iota(jnp.int32, (256, 256), 1)
    c2 = SCALE * LOG2E

    def softmax(qb, carry):
        for head in range(2):
            n = qb * 2 + head
            cols = slice(128 * head, 128 * head + 128)
            queries = qbuf[qb, :, cols]
            dout = dobuf[qb, :, cols]
            top = jnp.full((1, 256), NEG, F32)
            for jj in range(5):
                s = dot_nt(kvbuf[0, qb + jj], queries)
                if jj == 0:
                    s = jnp.where(key_row > query_col, s, NEG)
                if jj == 4:
                    s = jnp.where(key_row <= query_col, s, NEG)
                pbuf[n, jj] = s
                there = 2 * c + qb + jj >= 4
                top = jnp.maximum(
                    top, jnp.where(there, jnp.max(s, axis=0, keepdims=True), NEG)
                )
            top = top * c2
            total = jnp.zeros((1, 256), F32)
            delta = jnp.zeros((1, 256), F32)
            for jj in range(5):
                there = 2 * c + qb + jj >= 4
                p = jnp.exp2(pbuf[n, jj] * c2 - jnp.where(there, top, -NEG))
                dp = dot_nt(kvbuf[1, qb + jj], dout)
                total = total + jnp.sum(p, axis=0, keepdims=True)
                delta = delta + jnp.sum(p * dp, axis=0, keepdims=True)
                pbuf[n, jj] = p
                dpbuf[n, jj] = dp
            inverse = 1.0 / total
            stats[n, 0:1] = inverse
            stats[n, 1:2] = delta * inverse
        return carry

    lax.fori_loop(0, 2, softmax, 0)

    def terms(j):
        dk = jnp.zeros((256, 128), F32)
        dv = jnp.zeros((256, 128), F32)
        for qb in range(2):
            jj = j - qb
            if jj < 0 or jj > 4:
                continue
            for head in range(2):
                n = qb * 2 + head
                cols = slice(128 * head, 128 * head + 128)
                p = pbuf[n, jj] * stats[n, 0:1]
                ds = (p * (dpbuf[n, jj] - stats[n, 1:2])).astype(BF16)
                dsbuf[n, jj] = ds
                dv = dv + dot_nn(p.astype(BF16), dobuf[qb, :, cols])
                dk = dk + dot_nn(ds, qbuf[qb, :, cols])
        return dk * SCALE, dv

    for j in (0, 2, 1, 3):
        dk, dv = terms(j)
        gsend[j, 0] = dk.astype(BF16)
        gsend[j, 1] = dv.astype(BF16)
        d, core = 2 - j // 2, j % 2
        send(
            gsend.at[j], grecv.at[d - 1, e], gr_s.at[j], gr_r.at[(d - 1) * 2 + e], chip(-d, core)
        )
    for core in range(2):
        dk, dv = terms(4 + core)
        ownf[core, 0] = dk
        ownf[core, 1] = dv
    send(ownf.at[f], pbase, fin_s.at[0], fin_r.at[0], partner)
    for qb in range(2):
        for head in range(2):
            n = qb * 2 + head
            dq = jnp.zeros((256, 128), F32)
            for jj in range(5):
                dq = dq + dot_tn(dsbuf[n, jj], kvbuf[0, qb + jj])
            dqx[qb, :, 128 * head : 128 * head + 128] = dq * SCALE
    send(dqx.at[f], gq_out.at[:, lane(e, 256)], fin_s.at[1], fin_r.at[1], partner)
    gq_own = pltpu.make_async_copy(dqx.at[e], gq_out.at[:, lane(e, 256)], loc.at[6])
    gq_own.start()

    for which in range(2):
        ost[e, which] = ownf[e, which]
    arrive(pbase, fin_r.at[0])
    for which in range(2):
        ost[f, which] = pbase[which]
    outs = []
    for d in (1, 2):
        for core in range(2):
            arrive(grecv.at[d - 1, core], gr_r.at[(d - 1) * 2 + core])
    for core in range(2):
        for which, out in ((0, gk_out), (1, gv_out)):
            ost[core, which] = (
                ost[core, which]
                + grecv[0, core, which].astype(F32)
                + grecv[1, core, which].astype(F32)
            )
            copy = pltpu.make_async_copy(
                ost.at[core, which],
                out.at[:, 128 * core : 128 * core + 128],
                loc.at[7 + 2 * core + which],
            )
            copy.start()
            outs.append(copy)
    arrive(gq_out.at[:, lane(f, 256)], fin_r.at[1])
    gq_own.wait()
    for copy in outs:
        copy.wait()
    for copy in sends:
        copy.wait_send()


def on_device(chips, q, k, v, g, w):
    rows, width = q.shape
    kv_width = k.shape[1]
    model = g.shape[1]
    any_spec = pl.BlockSpec(memory_space=pl.ANY)
    dma = pltpu.SemaphoreType.DMA
    vmem = pltpu.VMEM
    return pl.pallas_call(
        functools.partial(kernel, chips),
        out_shape=(
            jax.ShapeDtypeStruct((rows, width), F32),
            jax.ShapeDtypeStruct((rows, kv_width), F32),
            jax.ShapeDtypeStruct((rows, kv_width), F32),
        ),
        in_specs=[any_spec] * 5,
        out_specs=[any_spec] * 3,
        scratch_shapes=[
            vmem((192, model), BF16),
            vmem((64, model), BF16),
            vmem((512, model), BF16),
            vmem((2, 256, 256), BF16),
            vmem((2, 256, 256), BF16),
            vmem((2, 256, 256), BF16),
            vmem((2, 6, 256, 128), BF16),
            vmem((4, 5, 256, 256), F32),
            vmem((4, 5, 256, 256), F32),
            vmem((4, 5, 256, 256), BF16),
            vmem((4, 8, 256), F32),
            vmem((4, 2, 256, 128), BF16),
            vmem((2, 2, 2, 256, 128), BF16),
            vmem((2, 2, 256, 128), F32),
            vmem((2, 256, 128), F32),
            vmem((2, 2, 256, 128), F32),
            vmem((2, 256, 256), F32),
            dma((12,)),
            dma((6,)),
            dma((6,)),
            dma((10,)),
            dma((10,)),
            dma((1,)),
            dma((1,)),
            dma((3,)),
            dma((3,)),
            dma((4,)),
            dma((4,)),
            dma((2,)),
            dma((2,)),
        ],
        compiler_params=pltpu.CompilerParams(
            collective_id=0, has_side_effects=True, vmem_limit_bytes=60 * 1024 * 1024
        ),
        name="band_grads",
    )(q, k, v, g, w)


def solution(mesh):
    in_specs = (
        P("ctx", "tp"),
        P("ctx", "tp"),
        P("ctx", "tp"),
        P(("ctx", "tp"), None),
        P("tp", None),
    )
    out_specs = (P("ctx", "tp"), P("ctx", "tp"), P("ctx", "tp"))
    chips = mesh.shape["ctx"] // 2
    return jax.shard_map(
        functools.partial(on_device, chips),
        mesh=mesh,
        in_specs=in_specs,
        out_specs=out_specs,
        check_vma=False,
    )
```

```python
import functools

import jax
import jax.numpy as jnp
from jax import lax
from jax.experimental import pallas as pl
from jax.experimental.pallas import tpu as pltpu
from jax.sharding import PartitionSpec as P

HD = 128
WIN = 1024
SCALE = 168.0 ** (-0.5)
LOG2E = 1.4426950408889634
NEG = -1e30
MESH = pl.DeviceIdType.MESH
ZHI, ZLO = 3, 4
F32 = jnp.float32
BF16 = jnp.bfloat16

ROWS = (
    ((96, 0, 160), (0, 160, 96), -1),
    ((32, 0, 224), (0, 224, 32), -1),
    ((0, 32, 224), (224, 0, 32), 1),
    ((0, 96, 160), (160, 0, 96), 1),
)


def dot_nt(a, b):
    return lax.dot_general(a, b, (((1,), (1,)), ((), ())), preferred_element_type=F32)


def dot_nn(a, b):
    return lax.dot_general(a, b, (((1,), (0,)), ((), ())), preferred_element_type=F32)


def dot_tn(a, b):
    return lax.dot_general(a, b, (((0,), (0,)), ((), ())), preferred_element_type=F32)


def kernel(
    chips, q_in, k_in, v_in, g_in, w_in, gq_out, base, grecv,
    main, relay, wbuf, ybuf, dobuf, qbuf, kvbuf, pbuf, dpbuf, dsbuf, stats,
    gsend, ownf, dqx,
    ready, loc, ag_s, ag_r, kv_s, kv_r, q_s, q_r, do_s, do_r, gr_s, gr_r, fin_s, fin_r,
):
    ctx = lax.axis_index("ctx")
    k = lax.axis_index("tp")
    e = lax.rem(ctx, 2)
    f = 1 - e
    c = ctx // 2
    r = c // ZHI
    zh = lax.rem(c, ZHI)
    z = zh * ZLO + k
    nz = ZHI * ZLO

    def plane(d, core):
        zz = lax.rem(z + d + nz, nz)
        return (((r * ZHI + zz // ZLO) * 2 + core), lax.rem(zz, ZLO))

    def group(d, core):
        return ((r * ZHI + lax.rem(zh + d + ZHI, ZHI)) * 2 + core, k)

    def chip(d, core):
        return (lax.rem(c + d + chips, chips) * 2 + core, k)

    partner = (c * 2 + f, k)

    def remote(src, dst, ss, rs, dev):
        return pltpu.make_async_remote_copy(
            src_ref=src, dst_ref=dst, send_sem=ss, recv_sem=rs, device_id=dev, device_id_type=MESH
        )

    def arrive(dst, rs):
        remote(dst, dst, rs, rs, partner).wait_recv()

    def lane(i, n):
        return pl.ds(pl.multiple_of(i * n, n), n)

    local = [
        pltpu.make_async_copy(g_in, main.at[64:128], loc.at[0]),
        pltpu.make_async_copy(w_in, wbuf, loc.at[1]),
        pltpu.make_async_copy(k_in.at[:, lane(e, 128)], kvbuf.at[0, 4 + e], loc.at[2]),
        pltpu.make_async_copy(v_in.at[:, lane(e, 128)], kvbuf.at[1, 4 + e], loc.at[3]),
        pltpu.make_async_copy(q_in.at[:, lane(e, 256)], qbuf.at[e], loc.at[4]),
    ]
    for copy in local:
        copy.start()

    barrier = pltpu.get_barrier_semaphore()

    def greet(dev):
        pl.semaphore_signal(barrier, inc=1, device_id=dev, device_id_type=MESH)

    back = jnp.where(k < 2, 1, -1)
    greet(partner)
    greet(plane(1, 1))
    greet(plane(-1, 1))
    greet(group(back, 0))
    for d in (1, 2, -1, -2):
        greet(chip(d, 0))

    sends = []

    def send(*args):
        copy = remote(*args)
        copy.start()
        sends.append(copy)

    @pl.when(e == 1)
    def _():
        pl.semaphore_wait(barrier, 5)
        pl.semaphore_signal(ready.at[0], inc=1, device_id=partner, device_id_type=MESH)

    @pl.when(e == 0)
    def _():
        pl.semaphore_wait(ready.at[0], 1)

    send(g_in.at[32:64], main.at[32:64], ag_s.at[0], ag_r.at[0], plane(1, e))
    send(g_in.at[0:32], main.at[128:160], ag_s.at[1], ag_r.at[1], plane(-1, e))
    send(g_in.at[0:32], main.at[0:32], ag_s.at[2], ag_r.at[2], plane(1, e))
    send(g_in.at[32:64], main.at[160:192], ag_s.at[3], ag_r.at[3], plane(-1, e))
    send(q_in.at[:, lane(f, 256)], qbuf.at[e], q_s.at[0], q_r.at[0], partner)
    send(k_in.at[:, lane(f, 128)], kvbuf.at[0, 4 + e], kv_s.at[0], kv_r.at[0], partner)
    send(v_in.at[:, lane(f, 128)], kvbuf.at[1, 4 + e], kv_s.at[1], kv_r.at[1], partner)
    arrive(main.at[32:64], ag_r.at[0])
    send(main.at[32:64], relay.at[0:32], ag_s.at[4], ag_r.at[4], plane(1, e))
    arrive(main.at[128:160], ag_r.at[1])
    send(main.at[128:160], relay.at[32:64], ag_s.at[5], ag_r.at[5], plane(-1, e))
    @pl.when(e == 0)
    def _():
        pl.semaphore_wait(barrier, 11)
        pl.semaphore_signal(ready.at[1], inc=1, device_id=partner, device_id_type=MESH)

    @pl.when(e == 1)
    def _():
        pl.semaphore_wait(ready.at[1], 1)

    for d in (1, 2):
        for core in range(2):
            for which, src in ((0, k_in), (1, v_in)):
                slot = 2 + (d - 1) * 4 + which
                send(
                    src.at[:, 128 * core : 128 * core + 128],
                    kvbuf.at[which, 4 - 2 * d + e],
                    kv_s.at[slot + 2 * core],
                    kv_r.at[slot + 2 * e],
                    chip(d, core),
                )

    for copy in local:
        copy.wait()
    arrive(main.at[0:32], ag_r.at[2])
    arrive(main.at[160:192], ag_r.at[3])
    for h in range(2):
        ybuf[h, 32:224] = dot_nt(main[...], wbuf[256 * h : 256 * h + 256]).astype(BF16)
    arrive(relay.at[0:32], ag_r.at[4])
    arrive(relay.at[32:64], ag_r.at[5])
    for h in range(2):
        ends = dot_nt(relay[...], wbuf[256 * h : 256 * h + 256]).astype(BF16)
        ybuf[h, 0:32] = ends[0:32]
        ybuf[h, 224:256] = ends[32:64]

    for case, (kept, moved, way) in enumerate(ROWS):
        src, home, count = kept
        msrc, mhome, mcount = moved

        def rows_out():
            copies = [
                remote(
                    ybuf.at[core, msrc : msrc + mcount],
                    dobuf.at[e, mhome : mhome + mcount],
                    do_s.at[1 + core],
                    do_r.at[1 + e],
                    group(way, core),
                )
                for core in range(2)
            ]
            copies.append(
                remote(
                    ybuf.at[f, src : src + count],
                    dobuf.at[e, home : home + count],
                    do_s.at[0],
                    do_r.at[0],
                    partner,
                )
            )
            return copies

        @pl.when(k == case)
        def _():
            for copy in rows_out():
                copy.start()
            own = pltpu.make_async_copy(
                ybuf.at[e, src : src + count], dobuf.at[e, home : home + count], loc.at[5]
            )
            own.start()
            own.wait()
            arrive(dobuf.at[f, home : home + count], do_r.at[0])
            for core in range(2):
                arrive(dobuf.at[core, mhome : mhome + mcount], do_r.at[1 + core])
            for copy in rows_out():
                copy.wait_send()

    arrive(qbuf.at[f], q_r.at[0])
    for which in range(2):
        arrive(kvbuf.at[which, 4 + f], kv_r.at[which])
    for d in (1, 2):
        for core in range(2):
            for which in range(2):
                arrive(
                    kvbuf.at[which, 4 - 2 * d + core], kv_r.at[2 + (d - 1) * 4 + which + 2 * core]
                )

    key_row = lax.broadcasted_iota(jnp.int32, (256, 256), 0)
    query_col = lax.broadcasted_iota(jnp.int32, (256, 256), 1)
    c2 = SCALE * LOG2E

    def softmax(qb, carry):
        for head in range(2):
            n = qb * 2 + head
            cols = slice(128 * head, 128 * head + 128)
            queries = qbuf[qb, :, cols]
            dout = dobuf[qb, :, cols]
            top = jnp.full((1, 256), NEG, F32)
            for jj in range(5):
                s = dot_nt(kvbuf[0, qb + jj], queries)
                if jj == 0:
                    s = jnp.where(key_row > query_col, s, NEG)
                if jj == 4:
                    s = jnp.where(key_row <= query_col, s, NEG)
                pbuf[n, jj] = s
                there = 2 * c + qb + jj >= 4
                top = jnp.maximum(
                    top, jnp.where(there, jnp.max(s, axis=0, keepdims=True), NEG)
                )
            top = top * c2
            total = jnp.zeros((1, 256), F32)
            delta = jnp.zeros((1, 256), F32)
            for jj in range(5):
                there = 2 * c + qb + jj >= 4
                p = jnp.exp2(pbuf[n, jj] * c2 - jnp.where(there, top, -NEG))
                dp = dot_nt(kvbuf[1, qb + jj], dout)
                total = total + jnp.sum(p, axis=0, keepdims=True)
                delta = delta + jnp.sum(p * dp, axis=0, keepdims=True)
                pbuf[n, jj] = p
                dpbuf[n, jj] = dp
            inverse = 1.0 / total
            stats[n, 0:1] = inverse
            stats[n, 1:2] = delta * inverse
        return carry

    lax.fori_loop(0, 2, softmax, 0)

    def terms(j):
        dk = jnp.zeros((256, 128), F32)
        dv = jnp.zeros((256, 128), F32)
        for qb in range(2):
            jj = j - qb
            if jj < 0 or jj > 4:
                continue
            for head in range(2):
                n = qb * 2 + head
                cols = slice(128 * head, 128 * head + 128)
                p = pbuf[n, jj] * stats[n, 0:1]
                ds = (p * (dpbuf[n, jj] - stats[n, 1:2])).astype(BF16)
                dsbuf[n, jj] = ds
                dv = dv + dot_nn(p.astype(BF16), dobuf[qb, :, cols])
                dk = dk + dot_nn(ds, qbuf[qb, :, cols])
        return dk * SCALE, dv

    for j in (0, 2, 1, 3):
        dk, dv = terms(j)
        gsend[j, 0] = dk.astype(BF16)
        gsend[j, 1] = dv.astype(BF16)
        d, core = 2 - j // 2, j % 2
        send(
            gsend.at[j], grecv.at[d - 1, e], gr_s.at[j], gr_r.at[(d - 1) * 2 + e], chip(-d, core)
        )
    for core in range(2):
        dk, dv = terms(4 + core)
        ownf[core, 0] = dk
        ownf[core, 1] = dv
    send(ownf.at[f], base.at[e], fin_s.at[0], fin_r.at[0], partner)
    kept = [pltpu.make_async_copy(ownf.at[e], base.at[e], loc.at[7])]
    kept[0].start()
    for qb in range(2):
        for head in range(2):
            n = qb * 2 + head
            dq = jnp.zeros((256, 128), F32)
            for jj in range(5):
                dq = dq + dot_tn(dsbuf[n, jj], kvbuf[0, qb + jj])
            dqx[qb, :, 128 * head : 128 * head + 128] = dq * SCALE
    send(dqx.at[f], gq_out.at[:, lane(e, 256)], fin_s.at[1], fin_r.at[1], partner)
    kept.append(pltpu.make_async_copy(dqx.at[e], gq_out.at[:, lane(e, 256)], loc.at[6]))
    kept[1].start()
    for copy in kept:
        copy.wait()
    arrive(base.at[f], fin_r.at[0])
    arrive(gq_out.at[:, lane(f, 256)], fin_r.at[1])
    for d in (1, 2):
        for core in range(2):
            arrive(grecv.at[d - 1, core], gr_r.at[(d - 1) * 2 + core])
    for copy in sends:
        copy.wait_send()


def finish(gq_in, base_in, grecv_in, gq_out, gk_out, gv_out, gq, base, grecv, ost, sems):
    loads = [
        pltpu.make_async_copy(base_in, base, sems.at[0]),
        pltpu.make_async_copy(grecv_in, grecv, sems.at[1]),
        pltpu.make_async_copy(gq_in, gq, sems.at[2]),
    ]
    for copy in loads:
        copy.start()
    loads[2].wait()
    outs = [pltpu.make_async_copy(gq, gq_out, sems.at[3])]
    outs[0].start()
    loads[0].wait()
    loads[1].wait()
    for which, out in ((0, gk_out), (1, gv_out)):
        for h in range(2):
            ost[which, :, 128 * h : 128 * h + 128] = (
                base[h, which] + grecv[0, h, which].astype(F32) + grecv[1, h, which].astype(F32)
            )
        copy = pltpu.make_async_copy(ost.at[which], out, sems.at[4 + which])
        copy.start()
        outs.append(copy)
    for copy in outs:
        copy.wait()


def on_device(chips, q, k, v, g, w):
    rows, width = q.shape
    kv_width = k.shape[1]
    model = g.shape[1]
    any_spec = pl.BlockSpec(memory_space=pl.ANY)
    dma = pltpu.SemaphoreType.DMA
    vmem = pltpu.VMEM
    gq, base, grecv = pl.pallas_call(
        functools.partial(kernel, chips),
        out_shape=(
            jax.ShapeDtypeStruct((rows, width), F32),
            jax.ShapeDtypeStruct((2, 2, 256, 128), F32),
            jax.ShapeDtypeStruct((2, 2, 2, 256, 128), BF16),
        ),
        in_specs=[any_spec] * 5,
        out_specs=[any_spec] * 3,
        scratch_shapes=[
            vmem((192, model), BF16),
            vmem((64, model), BF16),
            vmem((512, model), BF16),
            vmem((2, 256, 256), BF16),
            vmem((2, 256, 256), BF16),
            vmem((2, 256, 256), BF16),
            vmem((2, 6, 256, 128), BF16),
            vmem((4, 5, 256, 256), F32),
            vmem((4, 5, 256, 256), F32),
            vmem((4, 5, 256, 256), BF16),
            vmem((4, 8, 256), F32),
            vmem((4, 2, 256, 128), BF16),
            vmem((2, 2, 256, 128), F32),
            vmem((2, 256, 256), F32),
            pltpu.SemaphoreType.REGULAR((2,)),
            dma((12,)),
            dma((6,)),
            dma((6,)),
            dma((10,)),
            dma((10,)),
            dma((1,)),
            dma((1,)),
            dma((3,)),
            dma((3,)),
            dma((4,)),
            dma((4,)),
            dma((2,)),
            dma((2,)),
        ],
        compiler_params=pltpu.CompilerParams(
            collective_id=0, has_side_effects=True, vmem_limit_bytes=60 * 1024 * 1024
        ),
        name="band_grads",
    )(q, k, v, g, w)
    return pl.pallas_call(
        finish,
        out_shape=(
            jax.ShapeDtypeStruct((rows, width), F32),
            jax.ShapeDtypeStruct((rows, kv_width), F32),
            jax.ShapeDtypeStruct((rows, kv_width), F32),
        ),
        in_specs=[any_spec] * 3,
        out_specs=[any_spec] * 3,
        scratch_shapes=[
            vmem((rows, width), F32),
            vmem((2, 2, 256, 128), F32),
            vmem((2, 2, 2, 256, 128), BF16),
            vmem((2, rows, kv_width), F32),
            dma((6,)),
        ],
        name="finish",
    )(gq, base, grecv)


def solution(mesh):
    in_specs = (
        P("ctx", "tp"),
        P("ctx", "tp"),
        P("ctx", "tp"),
        P(("ctx", "tp"), None),
        P("tp", None),
    )
    out_specs = (P("ctx", "tp"), P("ctx", "tp"), P("ctx", "tp"))
    chips = mesh.shape["ctx"] // 2
    return jax.shard_map(
        functools.partial(on_device, chips),
        mesh=mesh,
        in_specs=in_specs,
        out_specs=out_specs,
        check_vma=False,
    )
```

```python
import functools

import jax
import jax.numpy as jnp
from jax import lax
from jax.experimental import pallas as pl
from jax.experimental.pallas import tpu as pltpu
from jax.sharding import PartitionSpec as P

HD = 128
WIN = 1024
SCALE = 168.0 ** (-0.5)
LOG2E = 1.4426950408889634
NEG = -1e30
MESH = pl.DeviceIdType.MESH
ZHI, ZLO = 3, 4
F32 = jnp.float32
BF16 = jnp.bfloat16

ROWS = (
    ((96, 0, 160), (0, 160, 96), -1),
    ((32, 0, 224), (0, 224, 32), -1),
    ((0, 32, 224), (224, 0, 32), 1),
    ((0, 96, 160), (160, 0, 96), 1),
)


def dot_nt(a, b):
    return lax.dot_general(a, b, (((1,), (1,)), ((), ())), preferred_element_type=F32)


def dot_nn(a, b):
    return lax.dot_general(a, b, (((1,), (0,)), ((), ())), preferred_element_type=F32)


def dot_tn(a, b):
    return lax.dot_general(a, b, (((0,), (0,)), ((), ())), preferred_element_type=F32)


def kernel(
    chips, q_in, k_in, v_in, g_in, w_in, gq_out, base, grecv,
    main, relay, wbuf, ybuf, dobuf, qbuf, kvbuf, pbuf, dpbuf, dsbuf, stats,
    gsend, ownf, dqx,
    ready, loc, ag_s, ag_r, kv_s, kv_r, q_s, q_r, do_s, do_r, gr_s, gr_r, fin_s, fin_r,
):
    ctx = lax.axis_index("ctx")
    k = lax.axis_index("tp")
    e = lax.rem(ctx, 2)
    f = 1 - e
    c = ctx // 2
    r = c // ZHI
    zh = lax.rem(c, ZHI)
    z = zh * ZLO + k
    nz = ZHI * ZLO

    def plane(d, core):
        zz = lax.rem(z + d + nz, nz)
        return (((r * ZHI + zz // ZLO) * 2 + core), lax.rem(zz, ZLO))

    def group(d, core):
        return ((r * ZHI + lax.rem(zh + d + ZHI, ZHI)) * 2 + core, k)

    def chip(d, core):
        return (lax.rem(c + d + chips, chips) * 2 + core, k)

    partner = (c * 2 + f, k)

    def remote(src, dst, ss, rs, dev):
        return pltpu.make_async_remote_copy(
            src_ref=src, dst_ref=dst, send_sem=ss, recv_sem=rs, device_id=dev, device_id_type=MESH
        )

    def arrive(dst, rs):
        remote(dst, dst, rs, rs, partner).wait_recv()

    def lane(i, n):
        return pl.ds(pl.multiple_of(i * n, n), n)

    local = [
        pltpu.make_async_copy(g_in, main.at[64:128], loc.at[0]),
        pltpu.make_async_copy(w_in, wbuf, loc.at[1]),
        pltpu.make_async_copy(k_in.at[:, lane(e, 128)], kvbuf.at[0, 4 + e], loc.at[2]),
        pltpu.make_async_copy(v_in.at[:, lane(e, 128)], kvbuf.at[1, 4 + e], loc.at[3]),
        pltpu.make_async_copy(q_in.at[:, lane(e, 256)], qbuf.at[e], loc.at[4]),
    ]
    for copy in local:
        copy.start()

    barrier = pltpu.get_barrier_semaphore()

    def greet(dev):
        pl.semaphore_signal(barrier, inc=1, device_id=dev, device_id_type=MESH)

    back = jnp.where(k < 2, 1, -1)
    greet(partner)
    greet(plane(1, 1))
    greet(plane(-1, 1))
    greet(group(back, 0))
    for d in (1, 2, -1, -2):
        greet(chip(d, 0))

    sends = []

    def send(*args):
        copy = remote(*args)
        copy.start()
        sends.append(copy)

    @pl.when(e == 1)
    def _():
        pl.semaphore_wait(barrier, 5)
        pl.semaphore_signal(ready.at[0], inc=1, device_id=partner, device_id_type=MESH)

    @pl.when(e == 0)
    def _():
        pl.semaphore_wait(ready.at[0], 1)

    send(g_in.at[32:64], main.at[32:64], ag_s.at[0], ag_r.at[0], plane(1, e))
    send(g_in.at[0:32], main.at[128:160], ag_s.at[1], ag_r.at[1], plane(-1, e))
    send(g_in.at[0:32], main.at[0:32], ag_s.at[2], ag_r.at[2], plane(1, e))
    send(g_in.at[32:64], main.at[160:192], ag_s.at[3], ag_r.at[3], plane(-1, e))
    send(q_in.at[:, lane(f, 256)], qbuf.at[e], q_s.at[0], q_r.at[0], partner)
    send(k_in.at[:, lane(f, 128)], kvbuf.at[0, 4 + e], kv_s.at[0], kv_r.at[0], partner)
    send(v_in.at[:, lane(f, 128)], kvbuf.at[1, 4 + e], kv_s.at[1], kv_r.at[1], partner)
    arrive(main.at[32:64], ag_r.at[0])
    send(main.at[32:64], relay.at[0:32], ag_s.at[4], ag_r.at[4], plane(1, e))
    arrive(main.at[128:160], ag_r.at[1])
    send(main.at[128:160], relay.at[32:64], ag_s.at[5], ag_r.at[5], plane(-1, e))

    @pl.when(e == 0)
    def _():
        pl.semaphore_wait(barrier, 11)
        pl.semaphore_signal(ready.at[1], inc=1, device_id=partner, device_id_type=MESH)

    @pl.when(e == 1)
    def _():
        pl.semaphore_wait(ready.at[1], 1)

    passed = []
    for core in range(2):
        for d in (1, 2):
            for which, src in ((0, k_in), (1, v_in)):
                slot = 2 + (d - 1) * 4 + which
                passed.append(remote(
                    src.at[:, 128 * core : 128 * core + 128],
                    kvbuf.at[which, 4 - 2 * d + e],
                    kv_s.at[slot + 2 * core],
                    kv_r.at[slot + 2 * e],
                    chip(d, core),
                ))


    @pl.when((k == 0) | (k == 2) | (k == 3))
    def _():
        for copy in passed:
            copy.start()

    for copy in local:
        copy.wait()
    arrive(main.at[0:32], ag_r.at[2])
    arrive(main.at[160:192], ag_r.at[3])
    for h in range(2):
        ybuf[h, 32:224] = dot_nt(main[...], wbuf[256 * h : 256 * h + 256]).astype(BF16)
    arrive(relay.at[0:32], ag_r.at[4])
    arrive(relay.at[32:64], ag_r.at[5])
    for h in range(2):
        ends = dot_nt(relay[...], wbuf[256 * h : 256 * h + 256]).astype(BF16)
        ybuf[h, 0:32] = ends[0:32]
        ybuf[h, 224:256] = ends[32:64]

    def rows_out(case):
        (src, home, count), (msrc, mhome, mcount), way = ROWS[case]
        copies = [
            remote(
                ybuf.at[core, msrc : msrc + mcount],
                dobuf.at[e, mhome : mhome + mcount],
                do_s.at[1 + core],
                do_r.at[1 + e],
                group(way, core),
            )
            for core in range(2)
        ]
        copies.append(
            remote(
                ybuf.at[f, src : src + count],
                dobuf.at[e, home : home + count],
                do_s.at[0],
                do_r.at[0],
                partner,
            )
        )
        copies.append(
            pltpu.make_async_copy(
                ybuf.at[e, src : src + count], dobuf.at[e, home : home + count], loc.at[5]
            )
        )
        return copies

    for case in range(ZLO):

        @pl.when(k == case)
        def _():
            for copy in rows_out(case):
                copy.start()


    @pl.when((k == 1))
    def _():
        for copy in passed:
            copy.start()


    arrive(qbuf.at[f], q_r.at[0])
    for which in range(2):
        arrive(kvbuf.at[which, 4 + f], kv_r.at[which])
    for d in (1, 2):
        for core in range(2):
            for which in range(2):
                arrive(
                    kvbuf.at[which, 4 - 2 * d + core], kv_r.at[2 + (d - 1) * 4 + which + 2 * core]
                )

    key_row = lax.broadcasted_iota(jnp.int32, (256, 256), 0)
    query_col = lax.broadcasted_iota(jnp.int32, (256, 256), 1)
    c2 = SCALE * LOG2E

    def scores(qb, carry):
        for head in range(2):
            n = qb * 2 + head
            queries = qbuf[qb, :, 128 * head : 128 * head + 128]
            top = jnp.full((1, 256), NEG, F32)
            for jj in range(5):
                s = dot_nt(kvbuf[0, qb + jj], queries)
                if jj == 0:
                    s = jnp.where(key_row > query_col, s, NEG)
                if jj == 4:
                    s = jnp.where(key_row <= query_col, s, NEG)
                pbuf[n, jj] = s
                there = 2 * c + qb + jj >= 4
                top = jnp.maximum(
                    top, jnp.where(there, jnp.max(s, axis=0, keepdims=True), NEG)
                )
            top = top * c2
            total = jnp.zeros((1, 256), F32)
            for jj in range(5):
                there = 2 * c + qb + jj >= 4
                p = jnp.exp2(pbuf[n, jj] * c2 - jnp.where(there, top, -NEG))
                total = total + jnp.sum(p, axis=0, keepdims=True)
                pbuf[n, jj] = p
            stats[n, 0:1] = 1.0 / total
        return carry

    def deltas(qb, carry):
        for head in range(2):
            n = qb * 2 + head
            dout = dobuf[qb, :, 128 * head : 128 * head + 128]
            delta = jnp.zeros((1, 256), F32)
            for jj in range(5):
                dp = dot_nt(kvbuf[1, qb + jj], dout)
                delta = delta + jnp.sum(pbuf[n, jj] * dp, axis=0, keepdims=True)
                dpbuf[n, jj] = dp
            stats[n, 1:2] = delta * stats[n, 0:1]
        return carry

    lax.fori_loop(0, 2, scores, 0)

    for case in range(ZLO):

        @pl.when(k == case)
        def _():
            (src, home, count), (msrc, mhome, mcount), way = ROWS[case]
            copies = rows_out(case)
            copies[-1].wait()
            arrive(dobuf.at[f, home : home + count], do_r.at[0])
            for core in range(2):
                arrive(dobuf.at[core, mhome : mhome + mcount], do_r.at[1 + core])
            for copy in copies[:-1]:
                copy.wait_send()

    lax.fori_loop(0, 2, deltas, 0)

    def terms(j):
        dk = jnp.zeros((256, 128), F32)
        dv = jnp.zeros((256, 128), F32)
        for qb in range(2):
            jj = j - qb
            if jj < 0 or jj > 4:
                continue
            for head in range(2):
                n = qb * 2 + head
                cols = slice(128 * head, 128 * head + 128)
                p = pbuf[n, jj] * stats[n, 0:1]
                ds = (p * (dpbuf[n, jj] - stats[n, 1:2])).astype(BF16)
                dsbuf[n, jj] = ds
                dv = dv + dot_nn(p.astype(BF16), dobuf[qb, :, cols])
                dk = dk + dot_nn(ds, qbuf[qb, :, cols])
        return dk * SCALE, dv

    for j in (0, 2, 1, 3):
        dk, dv = terms(j)
        gsend[j, 0] = dk.astype(BF16)
        gsend[j, 1] = dv.astype(BF16)
        d, core = 2 - j // 2, j % 2
        send(
            gsend.at[j], grecv.at[d - 1, e], gr_s.at[j], gr_r.at[(d - 1) * 2 + e], chip(-d, core)
        )
    for core in range(2):
        dk, dv = terms(4 + core)
        ownf[core, 0] = dk
        ownf[core, 1] = dv
    send(ownf.at[f], base.at[e], fin_s.at[0], fin_r.at[0], partner)
    kept = [pltpu.make_async_copy(ownf.at[e], base.at[e], loc.at[7])]
    kept[0].start()
    for qb in range(2):
        for head in range(2):
            n = qb * 2 + head
            dq = jnp.zeros((256, 128), F32)
            for jj in range(5):
                dq = dq + dot_tn(dsbuf[n, jj], kvbuf[0, qb + jj])
            dqx[qb, :, 128 * head : 128 * head + 128] = dq * SCALE
    send(dqx.at[f], gq_out.at[:, lane(e, 256)], fin_s.at[1], fin_r.at[1], partner)
    kept.append(pltpu.make_async_copy(dqx.at[e], gq_out.at[:, lane(e, 256)], loc.at[6]))
    kept[1].start()
    for copy in kept:
        copy.wait()
    arrive(base.at[f], fin_r.at[0])
    arrive(gq_out.at[:, lane(f, 256)], fin_r.at[1])
    for d in (1, 2):
        for core in range(2):
            arrive(grecv.at[d - 1, core], gr_r.at[(d - 1) * 2 + core])
    for copy in sends + passed:
        copy.wait_send()


def finish(gq_in, base_in, grecv_in, gq_out, gk_out, gv_out, gq, base, grecv, ost, sems):
    loads = [
        pltpu.make_async_copy(base_in, base, sems.at[0]),
        pltpu.make_async_copy(grecv_in, grecv, sems.at[1]),
        pltpu.make_async_copy(gq_in, gq, sems.at[2]),
    ]
    for copy in loads:
        copy.start()
    loads[2].wait()
    outs = [pltpu.make_async_copy(gq, gq_out, sems.at[3])]
    outs[0].start()
    loads[0].wait()
    loads[1].wait()
    for which, out in ((0, gk_out), (1, gv_out)):
        for h in range(2):
            ost[which, :, 128 * h : 128 * h + 128] = (
                base[h, which] + grecv[0, h, which].astype(F32) + grecv[1, h, which].astype(F32)
            )
        copy = pltpu.make_async_copy(ost.at[which], out, sems.at[4 + which])
        copy.start()
        outs.append(copy)
    for copy in outs:
        copy.wait()


def on_device(chips, q, k, v, g, w):
    rows, width = q.shape
    kv_width = k.shape[1]
    model = g.shape[1]
    any_spec = pl.BlockSpec(memory_space=pl.ANY)
    dma = pltpu.SemaphoreType.DMA
    vmem = pltpu.VMEM
    gq, base, grecv = pl.pallas_call(
        functools.partial(kernel, chips),
        out_shape=(
            jax.ShapeDtypeStruct((rows, width), F32),
            jax.ShapeDtypeStruct((2, 2, 256, 128), F32),
            jax.ShapeDtypeStruct((2, 2, 2, 256, 128), BF16),
        ),
        in_specs=[any_spec] * 5,
        out_specs=[any_spec] * 3,
        scratch_shapes=[
            vmem((192, model), BF16),
            vmem((64, model), BF16),
            vmem((512, model), BF16),
            vmem((2, 256, 256), BF16),
            vmem((2, 256, 256), BF16),
            vmem((2, 256, 256), BF16),
            vmem((2, 6, 256, 128), BF16),
            vmem((4, 5, 256, 256), F32),
            vmem((4, 5, 256, 256), F32),
            vmem((4, 5, 256, 256), BF16),
            vmem((4, 8, 256), F32),
            vmem((4, 2, 256, 128), BF16),
            vmem((2, 2, 256, 128), F32),
            vmem((2, 256, 256), F32),
            pltpu.SemaphoreType.REGULAR((2,)),
            dma((12,)),
            dma((6,)),
            dma((6,)),
            dma((10,)),
            dma((10,)),
            dma((1,)),
            dma((1,)),
            dma((3,)),
            dma((3,)),
            dma((4,)),
            dma((4,)),
            dma((2,)),
            dma((2,)),
        ],
        compiler_params=pltpu.CompilerParams(
            collective_id=0, has_side_effects=True, vmem_limit_bytes=60 * 1024 * 1024
        ),
        name="band_grads",
    )(q, k, v, g, w)
    return pl.pallas_call(
        finish,
        out_shape=(
            jax.ShapeDtypeStruct((rows, width), F32),
            jax.ShapeDtypeStruct((rows, kv_width), F32),
            jax.ShapeDtypeStruct((rows, kv_width), F32),
        ),
        in_specs=[any_spec] * 3,
        out_specs=[any_spec] * 3,
        scratch_shapes=[
            vmem((rows, width), F32),
            vmem((2, 2, 256, 128), F32),
            vmem((2, 2, 2, 256, 128), BF16),
            vmem((2, rows, kv_width), F32),
            dma((6,)),
        ],
        name="finish",
    )(gq, base, grecv)


def solution(mesh):
    in_specs = (
        P("ctx", "tp"),
        P("ctx", "tp"),
        P("ctx", "tp"),
        P(("ctx", "tp"), None),
        P("tp", None),
    )
    out_specs = (P("ctx", "tp"), P("ctx", "tp"), P("ctx", "tp"))
    chips = mesh.shape["ctx"] // 2
    return jax.shard_map(
        functools.partial(on_device, chips),
        mesh=mesh,
        in_specs=in_specs,
        out_specs=out_specs,
        check_vma=False,
    )
```

```python
import functools

import jax
import jax.numpy as jnp
from jax import lax
from jax.experimental import pallas as pl
from jax.experimental.pallas import tpu as pltpu
from jax.sharding import PartitionSpec as P

HD = 128
WIN = 1024
SCALE = 168.0 ** (-0.5)
LOG2E = 1.4426950408889634
NEG = -1e30
MESH = pl.DeviceIdType.MESH
ZHI, ZLO = 3, 4
F32 = jnp.float32
BF16 = jnp.bfloat16

ROWS = (
    ((96, 0, 160), (0, 160, 96), -1),
    ((32, 0, 224), (0, 224, 32), -1),
    ((0, 32, 224), (224, 0, 32), 1),
    ((0, 96, 160), (160, 0, 96), 1),
)


def dot_nt(a, b):
    return lax.dot_general(a, b, (((1,), (1,)), ((), ())), preferred_element_type=F32)


def dot_nn(a, b):
    return lax.dot_general(a, b, (((1,), (0,)), ((), ())), preferred_element_type=F32)


def dot_tn(a, b):
    return lax.dot_general(a, b, (((0,), (0,)), ((), ())), preferred_element_type=F32)


def kernel(
    chips, q_in, k_in, v_in, g_in, w_in, gq_out, base, grecv,
    main, relay, wbuf, ybuf, dobuf, qbuf, kvbuf, pbuf, dpbuf, dsbuf, stats,
    gsend, ownf, dqx,
    ready, loc, ag_s, ag_r, kv_s, kv_r, q_s, q_r, do_s, do_r, gr_s, gr_r, fin_s, fin_r,
):
    ctx = lax.axis_index("ctx")
    k = lax.axis_index("tp")
    e = lax.rem(ctx, 2)
    f = 1 - e
    c = ctx // 2
    r = c // ZHI
    zh = lax.rem(c, ZHI)
    z = zh * ZLO + k
    nz = ZHI * ZLO

    def plane(d, core):
        zz = lax.rem(z + d + nz, nz)
        return (((r * ZHI + zz // ZLO) * 2 + core), lax.rem(zz, ZLO))

    def group(d, core):
        return ((r * ZHI + lax.rem(zh + d + ZHI, ZHI)) * 2 + core, k)

    def chip(d, core):
        return (lax.rem(c + d + chips, chips) * 2 + core, k)

    partner = (c * 2 + f, k)

    def remote(src, dst, ss, rs, dev):
        return pltpu.make_async_remote_copy(
            src_ref=src, dst_ref=dst, send_sem=ss, recv_sem=rs, device_id=dev, device_id_type=MESH
        )

    def arrive(dst, rs):
        remote(dst, dst, rs, rs, partner).wait_recv()

    barrier = pltpu.get_barrier_semaphore()

    def greet(dev):
        pl.semaphore_signal(barrier, inc=1, device_id=dev, device_id_type=MESH)

    back = jnp.where(k < 2, 1, -1)
    greet(partner)
    greet(plane(1, 1))
    greet(plane(-1, 1))
    greet(group(back, 0))
    for d in (1, 2, -1, -2):
        greet(chip(d, 0))

    sends = []

    def send(*args):
        copy = remote(*args)
        copy.start()
        sends.append(copy)

    def lane(i, n):
        return pl.ds(pl.multiple_of(i * n, n), n)

    local = [
        pltpu.make_async_copy(g_in, main.at[64:128], loc.at[0]),
        pltpu.make_async_copy(w_in, wbuf, loc.at[1]),
        pltpu.make_async_copy(k_in.at[:, lane(e, 128)], kvbuf.at[0, 4 + e], loc.at[2]),
        pltpu.make_async_copy(v_in.at[:, lane(e, 128)], kvbuf.at[1, 4 + e], loc.at[3]),
        pltpu.make_async_copy(q_in.at[:, lane(e, 256)], qbuf.at[e], loc.at[4]),
    ]
    for copy in local:
        copy.start()

    @pl.when(e == 1)
    def _():
        pl.semaphore_wait(barrier, 5)
        pl.semaphore_signal(ready.at[0], inc=1, device_id=partner, device_id_type=MESH)

    @pl.when(e == 0)
    def _():
        pl.semaphore_wait(ready.at[0], 1)

    send(g_in.at[32:64], main.at[32:64], ag_s.at[0], ag_r.at[0], plane(1, e))
    send(g_in.at[0:32], main.at[128:160], ag_s.at[1], ag_r.at[1], plane(-1, e))
    send(g_in.at[0:32], main.at[0:32], ag_s.at[2], ag_r.at[2], plane(1, e))
    send(g_in.at[32:64], main.at[160:192], ag_s.at[3], ag_r.at[3], plane(-1, e))
    send(q_in.at[:, lane(f, 256)], qbuf.at[e], q_s.at[0], q_r.at[0], partner)
    send(k_in.at[:, lane(f, 128)], kvbuf.at[0, 4 + e], kv_s.at[0], kv_r.at[0], partner)
    send(v_in.at[:, lane(f, 128)], kvbuf.at[1, 4 + e], kv_s.at[1], kv_r.at[1], partner)
    arrive(main.at[32:64], ag_r.at[0])
    send(main.at[32:64], relay.at[0:32], ag_s.at[4], ag_r.at[4], plane(1, e))
    arrive(main.at[128:160], ag_r.at[1])
    send(main.at[128:160], relay.at[32:64], ag_s.at[5], ag_r.at[5], plane(-1, e))

    @pl.when(e == 0)
    def _():
        pl.semaphore_wait(barrier, 11)
        pl.semaphore_signal(ready.at[1], inc=1, device_id=partner, device_id_type=MESH)

    @pl.when(e == 1)
    def _():
        pl.semaphore_wait(ready.at[1], 1)

    passed = []
    for core in range(2):
        for d in (1, 2):
            for which, src in ((0, k_in), (1, v_in)):
                slot = 2 + (d - 1) * 4 + which
                passed.append(remote(
                    src.at[:, 128 * core : 128 * core + 128],
                    kvbuf.at[which, 4 - 2 * d + e],
                    kv_s.at[slot + 2 * core],
                    kv_r.at[slot + 2 * e],
                    chip(d, core),
                ))


    @pl.when((k == 0) | (k == 2) | (k == 3))
    def _():
        for copy in passed:
            copy.start()

    for copy in local:
        copy.wait()
    arrive(main.at[0:32], ag_r.at[2])
    arrive(main.at[160:192], ag_r.at[3])
    for h in range(2):
        ybuf[h, 32:224] = dot_nt(main[...], wbuf[256 * h : 256 * h + 256]).astype(BF16)
    arrive(relay.at[0:32], ag_r.at[4])
    arrive(relay.at[32:64], ag_r.at[5])
    for h in range(2):
        ends = dot_nt(relay[...], wbuf[256 * h : 256 * h + 256]).astype(BF16)
        ybuf[h, 0:32] = ends[0:32]
        ybuf[h, 224:256] = ends[32:64]

    def rows_out(case):
        (src, home, count), (msrc, mhome, mcount), way = ROWS[case]
        copies = [
            remote(
                ybuf.at[core, msrc : msrc + mcount],
                dobuf.at[e, mhome : mhome + mcount],
                do_s.at[1 + core],
                do_r.at[1 + e],
                group(way, core),
            )
            for core in range(2)
        ]
        copies.append(
            remote(
                ybuf.at[f, src : src + count],
                dobuf.at[e, home : home + count],
                do_s.at[0],
                do_r.at[0],
                partner,
            )
        )
        copies.append(
            pltpu.make_async_copy(
                ybuf.at[e, src : src + count], dobuf.at[e, home : home + count], loc.at[5]
            )
        )
        return copies

    for case in range(ZLO):

        @pl.when(k == case)
        def _():
            for copy in rows_out(case):
                copy.start()


    @pl.when((k == 1))
    def _():
        for copy in passed:
            copy.start()


    arrive(qbuf.at[f], q_r.at[0])
    for which in range(2):
        arrive(kvbuf.at[which, 4 + f], kv_r.at[which])
    for d in (1, 2):
        for core in range(2):
            for which in range(2):
                arrive(
                    kvbuf.at[which, 4 - 2 * d + core], kv_r.at[2 + (d - 1) * 4 + which + 2 * core]
                )

    key_row = lax.broadcasted_iota(jnp.int32, (256, 256), 0)
    query_col = lax.broadcasted_iota(jnp.int32, (256, 256), 1)
    c2 = SCALE * LOG2E

    def scores(qb, carry):
        for head in range(2):
            n = qb * 2 + head
            queries = qbuf[qb, :, 128 * head : 128 * head + 128]
            top = jnp.full((1, 256), NEG, F32)
            for jj in range(5):
                s = dot_nt(kvbuf[0, qb + jj], queries)
                if jj == 0:
                    s = jnp.where(key_row > query_col, s, NEG)
                if jj == 4:
                    s = jnp.where(key_row <= query_col, s, NEG)
                pbuf[n, jj] = s
                there = 2 * c + qb + jj >= 4
                top = jnp.maximum(
                    top, jnp.where(there, jnp.max(s, axis=0, keepdims=True), NEG)
                )
            top = top * c2
            total = jnp.zeros((1, 256), F32)
            for jj in range(5):
                there = 2 * c + qb + jj >= 4
                p = jnp.exp2(pbuf[n, jj] * c2 - jnp.where(there, top, -NEG))
                total = total + jnp.sum(p, axis=0, keepdims=True)
                pbuf[n, jj] = p
            stats[n, 0:1] = 1.0 / total
        return carry

    def deltas(qb, carry):
        for head in range(2):
            n = qb * 2 + head
            dout = dobuf[qb, :, 128 * head : 128 * head + 128]
            delta = jnp.zeros((1, 256), F32)
            for jj in range(5):
                dp = dot_nt(kvbuf[1, qb + jj], dout)
                delta = delta + jnp.sum(pbuf[n, jj] * dp, axis=0, keepdims=True)
                dpbuf[n, jj] = dp
            stats[n, 1:2] = delta * stats[n, 0:1]
        return carry

    lax.fori_loop(0, 2, scores, 0)

    for case in range(ZLO):

        @pl.when(k == case)
        def _():
            (src, home, count), (msrc, mhome, mcount), way = ROWS[case]
            copies = rows_out(case)
            copies[-1].wait()
            arrive(dobuf.at[f, home : home + count], do_r.at[0])
            for core in range(2):
                arrive(dobuf.at[core, mhome : mhome + mcount], do_r.at[1 + core])
            for copy in copies[:-1]:
                copy.wait_send()

    lax.fori_loop(0, 2, deltas, 0)

    def terms(j):
        dk = jnp.zeros((256, 128), F32)
        dv = jnp.zeros((256, 128), F32)
        for qb in range(2):
            jj = j - qb
            if jj < 0 or jj > 4:
                continue
            for head in range(2):
                n = qb * 2 + head
                cols = slice(128 * head, 128 * head + 128)
                p = pbuf[n, jj] * stats[n, 0:1]
                ds = (p * (dpbuf[n, jj] - stats[n, 1:2])).astype(BF16)
                dsbuf[n, jj] = ds
                dv = dv + dot_nn(p.astype(BF16), dobuf[qb, :, cols])
                dk = dk + dot_nn(ds, qbuf[qb, :, cols])
        return dk * SCALE, dv

    for j in (0, 2, 1, 3):
        dk, dv = terms(j)
        gsend[j, 0] = dk.astype(BF16)
        gsend[j, 1] = dv.astype(BF16)
        d, core = 2 - j // 2, j % 2
        send(
            gsend.at[j], grecv.at[d - 1, e], gr_s.at[j], gr_r.at[(d - 1) * 2 + e], chip(-d, core)
        )
    for core in range(2):
        dk, dv = terms(4 + core)
        ownf[core, 0] = dk
        ownf[core, 1] = dv
    send(ownf.at[f], base.at[e], fin_s.at[0], fin_r.at[0], partner)
    kept = [pltpu.make_async_copy(ownf.at[e], base.at[e], loc.at[7])]
    kept[0].start()
    for qb in range(2):
        for head in range(2):
            n = qb * 2 + head
            dq = jnp.zeros((256, 128), F32)
            for jj in range(5):
                dq = dq + dot_tn(dsbuf[n, jj], kvbuf[0, qb + jj])
            dqx[qb, :, 128 * head : 128 * head + 128] = dq * SCALE
    send(dqx.at[f], gq_out.at[:, lane(e, 256)], fin_s.at[1], fin_r.at[1], partner)
    kept.append(pltpu.make_async_copy(dqx.at[e], gq_out.at[:, lane(e, 256)], loc.at[6]))
    kept[1].start()
    for copy in kept:
        copy.wait()
    arrive(base.at[f], fin_r.at[0])
    arrive(gq_out.at[:, lane(f, 256)], fin_r.at[1])
    for d in (1, 2):
        for core in range(2):
            arrive(grecv.at[d - 1, core], gr_r.at[(d - 1) * 2 + core])
    for copy in sends + passed:
        copy.wait_send()


def finish(gq_in, base_in, grecv_in, gq_out, gk_out, gv_out, gq, base, grecv, ost, sems):
    loads = []
    for which in range(2):
        loads.append(
            (
                pltpu.make_async_copy(base_in.at[:, which], base.at[:, which], sems.at[which]),
                pltpu.make_async_copy(
                    grecv_in.at[:, :, which], grecv.at[:, :, which], sems.at[2 + which]
                ),
            )
        )
    straight = pltpu.make_async_copy(gq_in, gq, sems.at[4])
    for pair in loads:
        for copy in pair:
            copy.start()
    straight.start()
    outs = []
    for which, out in ((0, gk_out), (1, gv_out)):
        for copy in loads[which]:
            copy.wait()
        for h in range(2):
            ost[which, :, 128 * h : 128 * h + 128] = (
                base[h, which] + grecv[0, h, which].astype(F32) + grecv[1, h, which].astype(F32)
            )
        outs.append(pltpu.make_async_copy(ost.at[which], out, sems.at[5 + which]))
        outs[-1].start()
    straight.wait()
    outs.append(pltpu.make_async_copy(gq, gq_out, sems.at[7]))
    outs[-1].start()
    for copy in outs:
        copy.wait()


def on_device(chips, q, k, v, g, w):
    rows, width = q.shape
    kv_width = k.shape[1]
    model = g.shape[1]
    any_spec = pl.BlockSpec(memory_space=pl.ANY)
    dma = pltpu.SemaphoreType.DMA
    vmem = pltpu.VMEM
    gq, base, grecv = pl.pallas_call(
        functools.partial(kernel, chips),
        out_shape=(
            jax.ShapeDtypeStruct((rows, width), F32),
            jax.ShapeDtypeStruct((2, 2, 256, 128), F32),
            jax.ShapeDtypeStruct((2, 2, 2, 256, 128), BF16),
        ),
        in_specs=[any_spec] * 5,
        out_specs=[any_spec] * 3,
        scratch_shapes=[
            vmem((192, model), BF16),
            vmem((64, model), BF16),
            vmem((512, model), BF16),
            vmem((2, 256, 256), BF16),
            vmem((2, 256, 256), BF16),
            vmem((2, 256, 256), BF16),
            vmem((2, 6, 256, 128), BF16),
            vmem((4, 5, 256, 256), F32),
            vmem((4, 5, 256, 256), F32),
            vmem((4, 5, 256, 256), BF16),
            vmem((4, 8, 256), F32),
            vmem((4, 2, 256, 128), BF16),
            vmem((2, 2, 256, 128), F32),
            vmem((2, 256, 256), F32),
            pltpu.SemaphoreType.REGULAR((2,)),
            dma((12,)),
            dma((6,)),
            dma((6,)),
            dma((10,)),
            dma((10,)),
            dma((1,)),
            dma((1,)),
            dma((3,)),
            dma((3,)),
            dma((4,)),
            dma((4,)),
            dma((2,)),
            dma((2,)),
        ],
        compiler_params=pltpu.CompilerParams(
            collective_id=0, has_side_effects=True, vmem_limit_bytes=60 * 1024 * 1024
        ),
        name="band_grads",
    )(q, k, v, g, w)
    return pl.pallas_call(
        finish,
        out_shape=(
            jax.ShapeDtypeStruct((rows, width), F32),
            jax.ShapeDtypeStruct((rows, kv_width), F32),
            jax.ShapeDtypeStruct((rows, kv_width), F32),
        ),
        in_specs=[any_spec] * 3,
        out_specs=[any_spec] * 3,
        scratch_shapes=[
            vmem((rows, width), F32),
            vmem((2, 2, 256, 128), F32),
            vmem((2, 2, 2, 256, 128), BF16),
            vmem((2, rows, kv_width), F32),
            dma((8,)),
        ],
        name="finish",
    )(gq, base, grecv)


def solution(mesh):
    in_specs = (
        P("ctx", "tp"),
        P("ctx", "tp"),
        P("ctx", "tp"),
        P(("ctx", "tp"), None),
        P("tp", None),
    )
    out_specs = (P("ctx", "tp"), P("ctx", "tp"), P("ctx", "tp"))
    chips = mesh.shape["ctx"] // 2
    return jax.shard_map(
        functools.partial(on_device, chips),
        mesh=mesh,
        in_specs=in_specs,
        out_specs=out_specs,
        check_vma=False,
    )
```
